256 devices in a mesh: gx: 16 (over y_hi, z), gy: 16 (over x, y_lo, core).
Axes of the slice: x: 4, y: 4 (y_hi: 2, y_lo: 2; y = y_hi * 2 + y_lo), z: 8, core: 2. Of those that a mesh axis runs over, the one named last changes fastest.
Arguments:
- low_res: bfloat16 [256, 256, 6, 128], P('gx', 'gy'), may hold values from -6 to 6
- kernel: bfloat16 [4, 4, 4, 64, 128], replicated, may hold values from -0.1875 to 0.1875
- bias: float32 [64], replicated, may hold values from -3 to 3
- cotangent: bfloat16 [512, 512, 6, 128], P('gx', 'gy'), may hold values from -6 to 6
Outputs:
- output: bfloat16 [512, 512, 6, 128], P('gx', 'gy')
- input_grad: bfloat16 [256, 256, 6, 128], P('gx', 'gy')
- kernel_grad: float32 [4, 4, 4, 64, 128], replicated
- bias_grad: float32 [64], replicated
The draws below stay inside these ranges and needn't reach their ends.
All inputs are finite; a program needn't handle non-finite values.
Results may differ from the reference program's by a relative error of at most 0.0085.
Values may be sent and summed in bfloat16 or wider, within the bound.
No kernel may reach another device: no remote copies, remote signals or barrier semaphores. Data moves between devices by JAX's collectives and lax.ppermute only.
A program may use at most 64 MiB of HBM per device.

```python
import jax
import jax.numpy as jnp
from jax import lax

CIN = 128
COUT = 64
NZ = 6
NX = 256
NY = 256


def level_of(stream_key, shape, cuts, least, high):
    gain, own = 1.0, jax.random.fold_in(stream_key, 6)
    for axis_at, parts in cuts:
        steps = jnp.exp(jax.random.uniform(jax.random.fold_in(own, axis_at), (parts,), jnp.float32, least / len(cuts), high / len(cuts)))
        gain = gain * jnp.repeat(steps, shape[axis_at] // parts).reshape([-1 if axis == axis_at else 1 for axis in range(len(shape))])
    return gain


def noise(key, shape, width, limit, cuts=(), kind=jnp.bfloat16):
    factor_of = level_of(key, shape, cuts, -0.22, 0.18) if cuts else 1.0
    array = jax.random.normal(key, shape, jnp.float32) * width * factor_of
    return jnp.minimum(jnp.maximum(array, -limit), limit).astype(kind)


def setup_inputs(seed: int = 0) -> dict:
    splits = jax.random.split(jax.random.key(seed), 5)
    return {
        "low_res": noise(splits[0], (NX, NY, NZ, CIN), 1.0, 6.0, ((0, 16), (1, 16))),
        "kernel": noise(splits[1], (4, 4, 4, COUT, CIN), (8 * CIN) ** -0.5, 0.1875),
        "bias": noise(splits[2], (COUT,), 0.5, 3.0, (), jnp.float32),
        "cotangent": noise(splits[3], (2 * NX, 2 * NY, NZ, 2 * COUT), 1.0, 6.0, ((0, 16), (1, 16))),
    }


SLOPE = 0.2
tap_table = ((1, 0, 3, -1), (2, 0, 0, 1))

def upsample(low_float, kernel_float):
    rows_x, rows_y, depth_cells, in_width = low_float.shape
    out_width = kernel_float.shape[3]
    padded = jnp.pad(low_float, ((1, 1), (1, 1), (1, 1), (0, 0)))
    parities = []
    for parity_x in range(2):
        for parity_y in range(2):
            for parity_z in range(2):
                total = jnp.zeros((rows_x, rows_y, depth_cells, out_width), jnp.float32)
                for pick_x in range(2):
                    tap_x = tap_table[parity_x][2 * pick_x]
                    off_x = tap_table[parity_x][2 * pick_x + 1]
                    for pick_y in range(2):
                        tap_y = tap_table[parity_y][2 * pick_y]
                        off_y = tap_table[parity_y][2 * pick_y + 1]
                        for pick_z in range(2):
                            tap_z = tap_table[parity_z][2 * pick_z]
                            off_z = tap_table[parity_z][2 * pick_z + 1]
                            piece = padded[1 + off_x:1 + off_x + rows_x, 1 + off_y:1 + off_y + rows_y, 1 + off_z:1 + off_z + depth_cells]
                            total = total + jnp.dot(piece, kernel_float[tap_x, tap_y, tap_z].T, preferred_element_type=jnp.float32, precision=lax.Precision.HIGHEST)
                parities.append(total)
    grid = jnp.stack(parities).reshape(2, 2, 2, rows_x, rows_y, depth_cells, out_width)
    grid = jnp.transpose(grid, (3, 0, 4, 1, 5, 2, 6))
    return grid.reshape(2 * rows_x, 2 * rows_y, depth_cells, 2 * out_width)

def reference(low_res, kernel, bias, cotangent):
    low_float = low_res.astype(jnp.float32)
    kernel_float = kernel.astype(jnp.float32)
    linear, pullback = jax.vjp(upsample, low_float, kernel_float)
    pre = linear + jnp.concatenate([bias, bias])
    output = jnp.where(pre > 0, pre, SLOPE * pre).astype(jnp.bfloat16)
    dpre = (cotangent.astype(jnp.float32) * jnp.where(pre > 0, 1.0, SLOPE)).astype(jnp.bfloat16)
    input_float, kernel_sum = pullback(dpre.astype(jnp.float32))
    input_grad = input_float.astype(jnp.bfloat16)
    kernel_grad = kernel_sum / NX
    bias_sum = lax.optimization_barrier(jnp.sum(dpre.astype(jnp.float32), axis=(0, 1, 2))).reshape(2, COUT)
    bias_grad = lax.optimization_barrier(jnp.sum(bias_sum, axis=0)) / NX
    return (output, input_grad, kernel_grad, bias_grad)
```

```python
import jax
import jax.numpy as jnp
from jax import lax
from jax.experimental import pallas as pl
from jax.experimental.pallas import tpu as pltpu
from jax.sharding import PartitionSpec as P

SLOPE = 0.2
F32 = jnp.float32
BF16 = jnp.bfloat16

TAP_X = ((2, 0), (3, 1))
TAP_Y = ((1, 3), (2, 0))
SHIFT_Y = ((1, 0), (1, 2))
TAP_Z = ((3, 1, None), (None, 2, 0))


def dot_nt(a, b):
    return lax.dot_general(a, b, (((1,), (1,)), ((), ())), preferred_element_type=F32)


def forward_body(low, ylo, yhi, xlo, xhi, kern, bias, cot, out, dpre, kgrad, bgrad, xf, xs, im, wt, c32, o32, dd, ddt):
    nx, nz, ny, ch = low.shape
    half = ch // 2
    rows = (nx + 1) * ny
    total = rows * nz

    for z in range(nz):
        xf[z, pl.ds(1, nx), 8:8 + ny, :] = low[:, z].astype(F32)
        xf[z, 0, 7:9 + ny, :] = xlo[z].astype(F32)
        xf[z, nx + 1, 7:9 + ny, :] = xhi[z].astype(F32)
    for x in range(nx):
        xf[:, 1 + x, 7, :] = ylo[x].astype(F32)
        xf[:, 1 + x, 8 + ny, :] = yhi[x].astype(F32)
    xs[:, 0] = jnp.zeros(xs.shape[:1] + xs.shape[2:], BF16)
    xs[:, nz + 1] = jnp.zeros(xs.shape[:1] + xs.shape[2:], BF16)

    def shift_step(z, carry):
        for s in range(3):
            xs[s, 1 + z] = xf[z, :, 7 + s:7 + s + ny, :].astype(BF16)
        return carry

    lax.fori_loop(0, nz, shift_step, 0)

    for py in range(2):
        for px in range(2):
            for c in range(2):
                row = px * ch + c * half
                for ux in range(2):
                    for vy in range(2):
                        for dz in range(3):
                            col = ((ux * 2 + vy) * 3 + dz) * ch
                            tz = TAP_Z[c][dz]
                            block = jnp.zeros((half, ch), BF16) if tz is None else kern[TAP_X[px][ux], TAP_Y[py][vy], tz]
                            wt[py, row:row + half, col:col + ch] = block

    pad = im.shape[1] - total
    im[:, total:, :] = jnp.zeros((2, pad, im.shape[2]), BF16)
    dd[:, total:, :] = jnp.zeros((2, pad, dd.shape[2]), BF16)
    bias_row = bias[...]

    def layer_step(z, acc):
        base = pl.multiple_of(z * rows, ny)
        c32[...] = cot[:, :, z].astype(F32)
        for py in range(2):
            for ux in range(2):
                for vy in range(2):
                    for dz in range(3):
                        col = ((ux * 2 + vy) * 3 + dz) * ch
                        im[py, pl.ds(base, rows), col:col + ch] = xs[SHIFT_Y[py][vy], z + dz, ux:ux + nx + 1].reshape(rows, ch)
            pre = dot_nt(im[py, pl.ds(base, rows), :], wt[py])
            dd[py, pl.ds(base, ny), 0:ch] = jnp.zeros((ny, ch), BF16)
            dd[py, pl.ds(base + nx * ny, ny), ch:2 * ch] = jnp.zeros((ny, ch), BF16)
            for q in range(2):
                part = pre[0:nx * ny, ch:2 * ch] if q == 0 else pre[ny:, 0:ch]
                part = part + bias_row
                up = part > 0
                cots = c32[:, q, pl.ds(py, ny, stride=2), :].reshape(nx * ny, ch)
                grad = (cots * jnp.where(up, 1.0, SLOPE)).astype(BF16)
                o32[:, q, pl.ds(py, ny, stride=2), :] = jnp.where(up, part, SLOPE * part).reshape(nx, ny, ch)
                if q == 0:
                    dd[py, pl.ds(base, nx * ny), ch:2 * ch] = grad
                else:
                    dd[py, pl.ds(base + ny, nx * ny), 0:ch] = grad
                dpre[py, :, q, z] = grad.reshape(nx, ny, ch)
                acc = acc + jnp.sum(grad.astype(F32).reshape(nx * ny // 8, 8, ch), axis=0)
        out[:, :, z] = o32[...].astype(BF16)
        return acc

    bgrad[...] = lax.fori_loop(0, nz, layer_step, jnp.zeros((8, ch), F32))

    for py in range(2):
        ddt[py] = dd[py].T
    for py in range(2):
        for block in range(im.shape[2] // (2 * ch)):
            terms = jnp.dot(ddt[py], im[py, :, block * 2 * ch:(block + 1) * 2 * ch], preferred_element_type=F32)
            for side in range(2):
                which = block * 2 + side
                ux, vy, dz = which // 6, which // 3 % 2, which % 3
                for px in range(2):
                    for c in range(2):
                        tz = TAP_Z[c][dz]
                        if tz is not None:
                            tap = (TAP_X[px][ux] * 4 + TAP_Y[py][vy]) * 4 + tz
                            row = px * ch + c * half
                            kgrad[tap] = terms[row:row + half, side * ch:(side + 1) * ch]


def run_forward(low, ylo, yhi, xlo, xhi, kern, bias_row, cot):
    nx, nz, ny, ch = low.shape
    rows = (nx + 1) * ny
    padded = -(-rows * nz // 128) * 128
    pairs = cot.reshape(nx, 2, nz, 2 * ny, ch)
    vmem = pl.BlockSpec(memory_space=pltpu.VMEM)
    out, dpre, kgrad, bgrad = pl.pallas_call(
        forward_body,
        out_shape=(
            jax.ShapeDtypeStruct((nx, 2, nz, 2 * ny, ch), BF16),
            jax.ShapeDtypeStruct((2, nx, 2, nz, ny, ch), BF16),
            jax.ShapeDtypeStruct((64, ch // 2, ch), F32),
            jax.ShapeDtypeStruct((8, ch), F32),
        ),
        in_specs=[vmem] * 8,
        out_specs=(vmem,) * 4,
        scratch_shapes=[
            pltpu.VMEM((nz, nx + 2, ny + 16, ch), F32),
            pltpu.VMEM((3, nz + 2, nx + 2, ny, ch), BF16),
            pltpu.VMEM((2, padded, 12 * ch), BF16),
            pltpu.VMEM((2, 2 * ch, 12 * ch), BF16),
            pltpu.VMEM((nx, 2, 2 * ny, ch), F32),
            pltpu.VMEM((nx, 2, 2 * ny, ch), F32),
            pltpu.VMEM((2, padded, 2 * ch), BF16),
            pltpu.VMEM((2, 2 * ch, padded), BF16),
        ],
        compiler_params=pltpu.CompilerParams(vmem_limit_bytes=56 << 20),
        cost_estimate=pl.CostEstimate(flops=12 * 2**30, bytes_accessed=8 << 20, transcendentals=0),
        name="forward",
    )(low, ylo, yhi, xlo, xhi, kern, bias_row, pairs)
    return out.reshape(2 * nx, nz, 2 * ny, ch), dpre.reshape(2, 2 * nx, nz, ny, ch), kgrad, bgrad


def backward_body(dpre, ylo, yhi, xlo, xhi, kern, grad, df, ds, wb):
    _, nx2, nz, ny, ch = dpre.shape
    nx = nx2 // 2
    half = ch // 2
    zero = jnp.zeros((nx + 1, 2, ny, ch), BF16)
    for var in range(4):
        ds[var, 0] = zero
        ds[var, nz + 1] = zero

    def layer_load(z, carry):
        for py in range(2):
            df[py, pl.ds(1, nx2), 8:8 + ny, :] = dpre[py, :, z].astype(F32)
            lead = 8 - py
            df[py, 0, lead:lead + ny + 1, :] = xlo[py, z].astype(F32)
            df[py, nx2 + 1, lead:lead + ny + 1, :] = xhi[py, z].astype(F32)
        df[0, pl.ds(1, nx2), 8 + ny:9 + ny, :] = yhi[z].astype(F32)
        df[1, pl.ds(1, nx2), 7:8, :] = ylo[z].astype(F32)
        for py in range(2):
            for vy in range(2):
                lead = 8 if vy == 0 else (9 if py == 0 else 7)
                ds[py * 2 + vy, 1 + z] = df[py, :, lead:lead + ny, :].astype(BF16).reshape(nx + 1, 2, ny, ch)
        return carry

    lax.fori_loop(0, nz, layer_load, 0)
    for py in range(2):
        for vy in range(2):
            for q in range(4):
                row = ((py * 2 + vy) * 4 + q) * 2 * ch
                ty = TAP_Y[py][vy]
                for place, tz in enumerate((1, 2, 3, 0)):
                    at = row + place * half
                    wb[at:at + half, :] = kern[q, ty, tz]
    lane = lax.broadcasted_iota(jnp.int32, (nx, ny, ch), 2)

    def layer_step(z, carry):
        acc = jnp.zeros((nx * ny, ch), F32)
        for var in range(4):
            pieces = []
            for q in range(4):
                same = ds[var, 1 + z, q // 2:q // 2 + nx, q % 2]
                above = ds[var, 2 + z, q // 2:q // 2 + nx, q % 2]
                below = ds[var, z, q // 2:q // 2 + nx, q % 2]
                mixed = jnp.where(lane < half, above.astype(F32), below.astype(F32)).astype(BF16)
                pieces += [same.reshape(nx * ny, ch), mixed.reshape(nx * ny, ch)]
            acc = acc + jnp.dot(jnp.concatenate(pieces, axis=1), wb[var * 8 * ch:(var + 1) * 8 * ch, :], preferred_element_type=F32)
        grad[:, z] = acc.astype(BF16).reshape(nx, ny, ch)
        return carry

    lax.fori_loop(0, nz, layer_step, 0)


def run_backward(dpre, ylo, yhi, xlo, xhi, kern):
    _, nx2, nz, ny, ch = dpre.shape
    vmem = pl.BlockSpec(memory_space=pltpu.VMEM)
    return pl.pallas_call(
        backward_body,
        out_shape=jax.ShapeDtypeStruct((nx2 // 2, nz, ny, ch), BF16),
        in_specs=[vmem] * 6,
        out_specs=vmem,
        scratch_shapes=[
            pltpu.VMEM((2, nx2 + 2, ny + 16, ch), F32),
            pltpu.VMEM((4, nz + 2, nx2 // 2 + 1, 2, ny, ch), BF16),
            pltpu.VMEM((32 * ch, ch), BF16),
        ],
        compiler_params=pltpu.CompilerParams(vmem_limit_bytes=40 << 20),
        cost_estimate=pl.CostEstimate(flops=4 * 2**30, bytes_accessed=4 << 20, transcendentals=0),
        name="backward",
    )(dpre, ylo, yhi, xlo, xhi, kern)


def from_lower(values, axis):
    count = lax.axis_size(axis)
    return lax.ppermute(values, axis, [(i, i + 1) for i in range(count - 1)])


def from_upper(values, axis):
    count = lax.axis_size(axis)
    return lax.ppermute(values, axis, [(i + 1, i) for i in range(count - 1)])


def exchanges():
    across, along = lax.axis_size("gx"), lax.axis_size("gy")
    steps = []
    bit = 1
    while bit < along:
        steps.append(("gy", bit))
        bit *= 2
    bit = 1
    while bit < across:
        steps.append(("gx", bit))
        bit *= 2
    wanted = [("gy", 1), ("gy", 4), ("gy", 2), ("gx", 1), ("gy", 8), ("gx", 8), ("gx", 2), ("gx", 4)]
    return [step for step in wanted if step in steps]


def swap(values, axis, bit):
    return lax.ppermute(values, axis, [(i, i ^ bit) for i in range(lax.axis_size(axis))])


def sum_over_devices(kgrad, brow):
    steps = exchanges()
    part = kgrad.reshape(-1, kgrad.shape[-1])
    extra = brow.reshape(1, -1)
    for at, (axis, bit) in enumerate(steps):
        half = part.shape[0] // 2
        up = (lax.axis_index(axis) & bit) != 0
        keep = jnp.where(up, part[half:], part[:half])
        give = jnp.where(up, part[:half], part[half:])
        if at < 3:
            high = extra.astype(BF16)
            low = (extra - high.astype(F32)).astype(BF16)
            tail = jnp.concatenate([jnp.broadcast_to(high, (8,) + high.shape[1:]), jnp.broadcast_to(low, (8,) + low.shape[1:])], axis=0)
            came = swap(jnp.concatenate([give.astype(BF16), tail], axis=0), axis, bit).astype(F32)
            extra = high.astype(F32) + low.astype(F32) + (came[half:half + 1] + came[half + 8:half + 9])
        else:
            tail = jnp.broadcast_to(extra, (8,) + extra.shape[1:])
            came = swap(jnp.concatenate([give, tail], axis=0), axis, bit)
            extra = extra + came[half:half + 1]
        part = keep + came[:half]
    grown = part.astype(BF16)
    for axis, bit in steps[::-1]:
        up = (lax.axis_index(axis) & bit) != 0
        came = swap(grown, axis, bit)
        grown = jnp.concatenate([jnp.where(up, came, grown), jnp.where(up, grown, came)], axis=0)
    return grown.astype(F32), extra


def per_device(low_res, kernel, bias, cotangent):
    low = jnp.transpose(low_res, (0, 2, 1, 3))
    cot = jnp.transpose(cotangent, (0, 2, 1, 3))
    nx, nz, ny, ch = low.shape
    bias_row = jnp.concatenate([bias, bias]).reshape(1, ch)
    ylo = from_lower(low[:, :, ny - 1], "gy")
    yhi = from_upper(low[:, :, 0], "gy")

    def with_corners(x):
        return jnp.concatenate([ylo[x][:, None], low[x], yhi[x][:, None]], axis=1)

    xlo = from_lower(with_corners(nx - 1), "gx")
    xhi = from_upper(with_corners(0), "gx")
    out, dpre, kgrad, bgrad = run_forward(low, ylo, yhi, xlo, xhi, kernel, bias_row, cot)
    kernel_sum, bias_sum = sum_over_devices(kgrad, jnp.sum(bgrad, axis=0))

    gyhi = from_upper(dpre[0, :, :, 0], "gy")
    gylo = from_lower(dpre[1, :, :, ny - 1], "gy")

    def grad_corners(x):
        even = jnp.concatenate([dpre[0, x], gyhi[x][:, None]], axis=1)
        odd = jnp.concatenate([gylo[x][:, None], dpre[1, x]], axis=1)
        return jnp.stack([even, odd])

    gxlo = from_lower(grad_corners(2 * nx - 1), "gx")
    gxhi = from_upper(grad_corners(0), "gx")
    tall = lambda a: jnp.transpose(a, (1, 0, 2))[:, :, None, :]
    grad = run_backward(dpre, tall(gylo), tall(gyhi), gxlo, gxhi, kernel)

    grid_rows = lax.axis_size("gx") * nx
    output = jnp.transpose(out, (0, 2, 1, 3))
    input_grad = jnp.transpose(grad, (0, 2, 1, 3))
    kernel_grad = kernel_sum.reshape(kernel.shape) / grid_rows
    bias_grad = jnp.sum(bias_sum.reshape(2, ch // 2), axis=0) / grid_rows
    return (output, input_grad, kernel_grad, bias_grad)


def solution(mesh):
    return jax.shard_map(
        per_device,
        mesh=mesh,
        in_specs=(P("gx", "gy", None, None), P(), P(), P("gx", "gy", None, None)),
        out_specs=(P("gx", "gy", None, None), P("gx", "gy", None, None), P(), P()),
        check_vma=False,
    )
```

```python
import jax
import jax.numpy as jnp
from jax import lax
from jax.experimental import pallas as pl
from jax.experimental.pallas import tpu as pltpu
from jax.sharding import PartitionSpec as P


SLOPE = 0.2
F32 = jnp.float32
BF16 = jnp.bfloat16

TAP_X = ((2, 0), (3, 1))
TAP_Y = ((1, 3), (2, 0))
SHIFT_Y = ((1, 0), (1, 2))
TAP_Z = ((3, 1, None), (None, 2, 0))


def dot_nt(a, b):
    return lax.dot_general(a, b, (((1,), (1,)), ((), ())), preferred_element_type=F32)


def forward_body(upper, low, ylo, yhi, xlo, xhi, kern, bias, cot, out, dpre, keep, give, bgrad, wt, xf, xs, im, c32, o32, ch32, dd, ddt, kgrad):
    nx, nz, ny, ch = low.shape
    half = ch // 2
    rows = (nx + 1) * ny
    total = rows * nz

    for z in range(nz):
        xf[z, pl.ds(1, nx), 8:8 + ny, :] = low[:, z].astype(F32)
        xf[z, 0, 7:9 + ny, :] = xlo[z, 2 * ny:3 * ny + 2].astype(F32)
        xf[z, nx + 1, 7:9 + ny, :] = xhi[z, 2 * ny:3 * ny + 2].astype(F32)
    for x in range(nx):
        xf[:, 1 + x, 7, :] = ylo[x].astype(F32)
        xf[:, 1 + x, 8 + ny, :] = yhi[x].astype(F32)
    xs[:, 0] = jnp.zeros(xs.shape[:1] + xs.shape[2:], BF16)
    xs[:, nz + 1] = jnp.zeros(xs.shape[:1] + xs.shape[2:], BF16)

    def shift_step(z, carry):
        for s in range(3):
            xs[s, 1 + z] = xf[z, :, 7 + s:7 + s + ny, :].astype(BF16)
        return carry

    lax.fori_loop(0, nz, shift_step, 0)

    for py in range(2):
        for px in range(2):
            for c in range(2):
                row = px * ch + c * half
                for ux in range(2):
                    for vy in range(2):
                        for dz in range(3):
                            col = ((ux * 2 + vy) * 3 + dz) * ch
                            tz = TAP_Z[c][dz]
                            block = jnp.zeros((half, ch), BF16) if tz is None else kern[TAP_X[px][ux], TAP_Y[py][vy], tz]
                            wt[py, row:row + half, col:col + ch] = block

    pad = im.shape[1] - total
    im[:, total:, :] = jnp.zeros((2, pad, im.shape[2]), BF16)
    dd[:, total:, :] = jnp.zeros((2, pad, dd.shape[2]), BF16)
    bias_row = bias[...]

    def layer_step(z, acc):
        base = pl.multiple_of(z * rows, ny)
        c32[...] = cot[:, :, z].astype(F32)
        ch32[0] = xlo[z, 0:2 * ny].astype(F32)
        ch32[1] = xhi[z, 0:2 * ny].astype(F32)
        for py in range(2):
            for ux in range(2):
                for vy in range(2):
                    for dz in range(3):
                        col = ((ux * 2 + vy) * 3 + dz) * ch
                        im[py, pl.ds(base, rows), col:col + ch] = xs[SHIFT_Y[py][vy], z + dz, ux:ux + nx + 1].reshape(rows, ch)
            pre = dot_nt(im[py, pl.ds(base, rows), :], wt[py])
            dd[py, pl.ds(base, ny), 0:ch] = jnp.zeros((ny, ch), BF16)
            dd[py, pl.ds(base + nx * ny, ny), ch:2 * ch] = jnp.zeros((ny, ch), BF16)
            for q in range(2):
                part = pre[0:nx * ny, ch:2 * ch] if q == 0 else pre[ny:, 0:ch]
                part = part + bias_row
                up = part > 0
                cots = c32[:, q, pl.ds(py, ny, stride=2), :].reshape(nx * ny, ch)
                grad = (cots * jnp.where(up, 1.0, SLOPE)).astype(BF16)
                o32[:, q, pl.ds(py, ny, stride=2), :] = jnp.where(up, part, SLOPE * part).reshape(nx, ny, ch)
                if q == 0:
                    dd[py, pl.ds(base, nx * ny), ch:2 * ch] = grad
                else:
                    dd[py, pl.ds(base + ny, nx * ny), 0:ch] = grad
                dpre[py, q:q + nx, 1 - q, z] = grad.reshape(nx, ny, ch)
                acc = acc + jnp.sum(grad.astype(F32).reshape(nx * ny // 8, 8, ch), axis=0)
            for side in range(2):
                part = (pre[0:ny, 0:ch] if side == 0 else pre[nx * ny:, ch:2 * ch]) + bias_row
                cots = ch32[side, pl.ds(py, ny, stride=2), :]
                dpre[py, side * nx, side, z] = (cots * jnp.where(part > 0, 1.0, SLOPE)).astype(BF16)
        out[:, :, z] = o32[...].astype(BF16)
        return acc

    sums = jnp.sum(lax.fori_loop(0, nz, layer_step, jnp.zeros((8, ch), F32)), axis=0, keepdims=True)
    high = sums.astype(BF16)
    rest = (sums - high.astype(F32)).astype(BF16)
    bgrad[...] = jnp.broadcast_to(high.astype(F32) + rest.astype(F32), bgrad.shape)

    for py in range(2):
        ddt[py] = dd[py].T
    for py in range(2):
        for block in range(im.shape[2] // (2 * ch)):
            terms = jnp.dot(ddt[py], im[py, :, block * 2 * ch:(block + 1) * 2 * ch], preferred_element_type=F32)
            for side in range(2):
                which = block * 2 + side
                ux, vy, dz = which // 6, which // 3 % 2, which % 3
                for px in range(2):
                    for c in range(2):
                        tz = TAP_Z[c][dz]
                        if tz is not None:
                            tx = TAP_X[px][ux]
                            at = (((tx % 2) * 4 + TAP_Y[py][vy]) * 4 + tz) * half
                            row = px * ch + c * half
                            kgrad[tx // 2, at:at + half] = terms[row:row + half, side * ch:(side + 1) * ch]
    mine = upper[0]
    taps = keep.shape[0]
    keep[...] = kgrad[mine]
    give[0:taps] = kgrad[1 - mine].astype(BF16)
    for k, extra in enumerate((high, rest)):
        give[taps + 8 * k:taps + 8 * k + 8] = jnp.broadcast_to(extra, (8, ch))


def run_forward(upper, low, ylo, yhi, xlo, xhi, kern, bias_row, cot):
    nx, nz, ny, ch = low.shape
    rows = (nx + 1) * ny
    padded = -(-rows * nz // 128) * 128
    pairs = cot.reshape(nx, 2, nz, 2 * ny, ch)
    vmem = pl.BlockSpec(memory_space=pltpu.VMEM)
    taps = 32 * ch // 2
    out, dpre, keep, give, bgrad, wt = pl.pallas_call(
        forward_body,
        out_shape=(
            jax.ShapeDtypeStruct((nx, 2, nz, 2 * ny, ch), BF16),
            jax.ShapeDtypeStruct((2, nx + 1, 2, nz, ny, ch), BF16),
            jax.ShapeDtypeStruct((taps, ch), F32),
            jax.ShapeDtypeStruct((taps + 16, ch), BF16),
            jax.ShapeDtypeStruct((8, ch), F32),
            jax.ShapeDtypeStruct((2, 2 * ch, 12 * ch), BF16),
        ),
        in_specs=[pl.BlockSpec(memory_space=pltpu.SMEM)] + [vmem] * 8,
        out_specs=(vmem,) * 6,
        scratch_shapes=[
            pltpu.VMEM((nz, nx + 2, ny + 16, ch), F32),
            pltpu.VMEM((3, nz + 2, nx + 2, ny, ch), BF16),
            pltpu.VMEM((2, padded, 12 * ch), BF16),
            pltpu.VMEM((nx, 2, 2 * ny, ch), F32),
            pltpu.VMEM((nx, 2, 2 * ny, ch), F32),
            pltpu.VMEM((2, 2 * ny, ch), F32),
            pltpu.VMEM((2, padded, 2 * ch), BF16),
            pltpu.VMEM((2, 2 * ch, padded), BF16),
            pltpu.VMEM((2, taps, ch), F32),
        ],
        compiler_params=pltpu.CompilerParams(vmem_limit_bytes=56 << 20),
        cost_estimate=pl.CostEstimate(flops=12 * 2**30, bytes_accessed=8 << 20, transcendentals=0),
        name="forward",
    )(upper, low, ylo, yhi, xlo, xhi, kern, bias_row, pairs)
    return out.reshape(2 * nx, nz, 2 * ny, ch), dpre, keep, give, bgrad, wt


def backward_body(dpre, cols, ccols, kern, bias, wt, grad, df, ds, wb, gh):
    _, duals, _, nz, ny, ch = dpre.shape
    nx = duals - 1
    half = ch // 2
    lanes = gh.shape[3]
    bias_row = bias[...]
    for py in range(2):
        pieces = []
        for ux in range(2):
            for vy in range(2):
                which = ((3, 2), (0, 1))[py][vy]
                for dz in range(3):
                    pieces.append(cols[which, dz:dz + nz, ux:ux + lanes, :].reshape(nz * lanes, ch).astype(BF16))
        pre = dot_nt(jnp.concatenate(pieces, axis=1), wt[py])
        for px in range(2):
            part = pre[:, px * ch:(px + 1) * ch] + bias_row
            cots = ccols[py, px].reshape(nz * lanes, ch)
            gh[py, px] = (cots * jnp.where(part > 0, 1.0, SLOPE)).astype(BF16).astype(F32).reshape(nz, lanes, ch)
    zero = jnp.zeros((nx + 1, 2, ny, ch), BF16)
    for var in range(4):
        ds[var, 0] = zero
        ds[var, nz + 1] = zero

    def layer_load(z, carry):
        for py in range(2):
            df[py, :, :, 8:8 + ny, :] = dpre[py, :, :, z].astype(F32)
            for px in range(2):
                df[py, :, px, 7 if py else 8 + ny, :] = gh[py, px, z, 0:nx + 1]
        for py in range(2):
            for vy in range(2):
                lead = 8 if vy == 0 else (9 if py == 0 else 7)
                ds[py * 2 + vy, 1 + z] = df[py, :, :, lead:lead + ny, :].astype(BF16)
        return carry

    lax.fori_loop(0, nz, layer_load, 0)
    for py in range(2):
        for vy in range(2):
            for q in range(4):
                row = ((py * 2 + vy) * 4 + q) * 2 * ch
                ty = TAP_Y[py][vy]
                for place, tz in enumerate((1, 2, 3, 0)):
                    at = row + place * half
                    wb[at:at + half, :] = kern[q, ty, tz]
    lane = lax.broadcasted_iota(jnp.int32, (nx, ny, ch), 2)

    def layer_step(z, carry):
        acc = jnp.zeros((nx * ny, ch), F32)
        for var in range(4):
            pieces = []
            for q in range(4):
                same = ds[var, 1 + z, q // 2:q // 2 + nx, q % 2]
                above = ds[var, 2 + z, q // 2:q // 2 + nx, q % 2]
                below = ds[var, z, q // 2:q // 2 + nx, q % 2]
                mixed = jnp.where(lane < half, above.astype(F32), below.astype(F32)).astype(BF16)
                pieces += [same.reshape(nx * ny, ch), mixed.reshape(nx * ny, ch)]
            acc = acc + jnp.dot(jnp.concatenate(pieces, axis=1), wb[var * 8 * ch:(var + 1) * 8 * ch, :], preferred_element_type=F32)
        grad[:, z] = acc.astype(BF16).reshape(nx, ny, ch)
        return carry

    lax.fori_loop(0, nz, layer_step, 0)


def run_backward(dpre, cols, ccols, kern, bias_row, wt):
    _, duals, _, nz, ny, ch = dpre.shape
    nx = duals - 1
    vmem = pl.BlockSpec(memory_space=pltpu.VMEM)
    return pl.pallas_call(
        backward_body,
        out_shape=jax.ShapeDtypeStruct((nx, nz, ny, ch), BF16),
        in_specs=[vmem] * 6,
        out_specs=vmem,
        scratch_shapes=[
            pltpu.VMEM((2, nx + 1, 2, ny + 16, ch), F32),
            pltpu.VMEM((4, nz + 2, nx + 1, 2, ny, ch), BF16),
            pltpu.VMEM((32 * ch, ch), BF16),
            pltpu.VMEM((2, 2, nz, nx + 8, ch), F32),
        ],
        compiler_params=pltpu.CompilerParams(vmem_limit_bytes=40 << 20),
        cost_estimate=pl.CostEstimate(flops=4 * 2**30, bytes_accessed=4 << 20, transcendentals=0),
        name="backward",
    )(dpre, cols, ccols, kern, bias_row, wt)


def from_both(first, last, axis):
    count = lax.axis_size(axis)
    odd = lax.axis_index(axis) % 2 == 1
    inner = lax.ppermute(jnp.where(odd, first, last), axis, [(i, i ^ 1) for i in range(count)])
    outer = lax.ppermute(jnp.where(odd, last, first), axis, [(i, i + 1 if i % 2 else i - 1) for i in range(1, count - 1)])
    return jnp.where(odd, inner, outer), jnp.where(odd, outer, inner)


HALVE = (("gy", 1), ("gy", 4), ("gy", 2), ("gy", 8))
GROUPS = (("gx", (1, 8, 9)), ("gx", (2, 4, 6)))


def swap(values, axis, bits):
    return lax.ppermute(values, axis, [(i, i ^ bits) for i in range(lax.axis_size(axis))])


def rounded(values):
    return lax.reduce_precision(values, 8, 7)


def with_extra(values, extra):
    high = rounded(extra)
    tail = [jnp.broadcast_to(part.astype(BF16), (8,) + part.shape[1:]) for part in (high, rounded(extra - high))]
    return jnp.concatenate([values.astype(BF16)] + tail, axis=0), high + rounded(extra - high)


def take_extra(message):
    rows = message.shape[0] - 16
    wide = message.astype(F32)
    return wide[:rows], wide[rows:rows + 1] + wide[rows + 8:rows + 9]


def sum_over_devices(keep, message, brow):
    steps = [(axis, bit) for axis, bit in HALVE if bit < lax.axis_size(axis)]
    groups = [(axis, [bits for bits in some if bits < lax.axis_size(axis)]) for axis, some in GROUPS]
    extra = brow[0:1]
    for at, (axis, bit) in enumerate(steps):
        if at:
            half = part.shape[0] // 2
            up = (lax.axis_index(axis) & bit) != 0
            keep = jnp.where(up, part[half:], part[:half])
            message, extra = with_extra(jnp.where(up, part[:half], part[half:]), extra)
        came, came_extra = take_extra(swap(message, axis, bit))
        part = keep + came
        extra = extra + came_extra
    for axis, some in groups:
        own = rounded(part)
        message, own_extra = with_extra(own, extra)
        arrived = [take_extra(swap(message, axis, bits)) for bits in some]
        if len(arrived) == 3:
            part = (own + arrived[0][0]) + (arrived[1][0] + arrived[2][0])
            extra = (own_extra + arrived[0][1]) + (arrived[1][1] + arrived[2][1])
        else:
            for more, more_extra in arrived:
                part, extra = own + more, own_extra + more_extra
    grown = part.astype(BF16)
    for axis, bit in steps[::-1]:
        up = (lax.axis_index(axis) & bit) != 0
        came = swap(grown, axis, bit)
        grown = jnp.concatenate([jnp.where(up, came, grown), jnp.where(up, grown, came)], axis=0)
    return grown.astype(F32), extra


def per_device(low_res, kernel, bias, cotangent):
    low = jnp.transpose(low_res, (0, 2, 1, 3))
    cot = jnp.transpose(cotangent, (0, 2, 1, 3))
    nx, nz, ny, ch = low.shape
    bias_row = jnp.concatenate([bias, bias]).reshape(1, ch)

    first = jnp.concatenate([low[:, :, 0], cot[:, :, 0]], axis=0)
    last = jnp.concatenate([low[:, :, ny - 1], cot[:, :, 2 * ny - 1]], axis=0)
    ylo, yhi = from_both(first, last, "gy")

    def row(cell, output):
        pieces = [cot[output], ylo[cell][:, None], low[cell], yhi[cell][:, None], ylo[nx + output][:, None], yhi[nx + output][:, None]]
        return jnp.concatenate(pieces, axis=1)

    xlo, xhi = from_both(row(0, 0), row(nx - 1, 2 * nx - 1), "gx")
    axis, bit = HALVE[0]
    upper = (lax.axis_index(axis) // bit % 2).astype(jnp.int32).reshape(1)
    out, dpre, keep, give, bgrad, wt = run_forward(upper, low, ylo, yhi, xlo, xhi, kernel, bias_row, cot)

    def column(at, middle):
        first, last = xlo[:, at][:, None], xhi[:, at][:, None]
        return jnp.concatenate([first, jnp.transpose(middle, (1, 0, 2)), last], axis=1)

    cols = jnp.stack([column(2 * ny, ylo[:nx]), column(2 * ny + 1, low[:, :, 0]), column(3 * ny, low[:, :, ny - 1]), column(3 * ny + 1, yhi[:nx])])
    cols = jnp.pad(cols.astype(F32), ((0, 0), (1, 1), (0, 14), (0, 0)))
    ccols = jnp.stack([column(3 * ny + 3, yhi[nx:]), column(3 * ny + 2, ylo[nx:])]).astype(F32)
    ccols = jnp.transpose(ccols.reshape(2, nz, nx + 1, 2, ch), (0, 3, 1, 2, 4))
    ccols = jnp.pad(ccols, ((0, 0), (0, 0), (0, 0), (0, 7), (0, 0)))
    grad = run_backward(dpre, cols, ccols, kernel, bias_row, wt)
    kernel_sum, bias_sum = sum_over_devices(keep, give, bgrad)

    grid_rows = lax.axis_size("gx") * nx
    output = jnp.transpose(out, (0, 2, 1, 3))
    input_grad = jnp.transpose(grad, (0, 2, 1, 3))
    kernel_grad = kernel_sum.reshape(kernel.shape) / grid_rows
    bias_grad = jnp.sum(bias_sum.reshape(2, ch // 2), axis=0) / grid_rows
    return (output, input_grad, kernel_grad, bias_grad)


def solution(mesh):
    return jax.shard_map(
        per_device,
        mesh=mesh,
        in_specs=(P("gx", "gy", None, None), P(), P(), P("gx", "gy", None, None)),
        out_specs=(P("gx", "gy", None, None), P("gx", "gy", None, None), P(), P()),
        check_vma=False,
    )
```

```python
import jax
import jax.numpy as jnp
from jax import lax
from jax.experimental import pallas as pl
from jax.experimental.pallas import tpu as pltpu
from jax.sharding import PartitionSpec as P


SLOPE = 0.2
F32 = jnp.float32
BF16 = jnp.bfloat16

TAP_X = ((2, 0), (3, 1))
TAP_Y = ((1, 3), (2, 0))
SHIFT_Y = ((1, 0), (1, 2))
TAP_Z = ((3, 1, None), (None, 2, 0))


def dot_nt(a, b):
    return lax.dot_general(a, b, (((1,), (1,)), ((), ())), preferred_element_type=F32)


def forward_body(upper, low, ylo, yhi, xlo, xhi, kern_in, bias, cot_in, out_to, dpre_to, keep, give, bgrad, wt_to, xf, xs, im, c32, o32, ch32, dd, ddt, kgrad, kern, cot, out, dpre, wt, sems):
    get_kern = pltpu.make_async_copy(kern_in, kern, sems.at[0])
    get_kern.start()
    get_cot = pltpu.make_async_copy(cot_in, cot, sems.at[1])
    get_cot.start()
    nx, nz, ny, ch = low.shape
    half = ch // 2
    rows = (nx + 1) * ny
    total = rows * nz

    for z in range(nz):
        xf[z, pl.ds(1, nx), 8:8 + ny, :] = low[:, z].astype(F32)
        xf[z, 0, 7:9 + ny, :] = xlo[z, 2 * ny:3 * ny + 2].astype(F32)
        xf[z, nx + 1, 7:9 + ny, :] = xhi[z, 2 * ny:3 * ny + 2].astype(F32)
    for x in range(nx):
        xf[:, 1 + x, 7, :] = ylo[x].astype(F32)
        xf[:, 1 + x, 8 + ny, :] = yhi[x].astype(F32)
    xs[:, 0] = jnp.zeros(xs.shape[:1] + xs.shape[2:], BF16)
    xs[:, nz + 1] = jnp.zeros(xs.shape[:1] + xs.shape[2:], BF16)

    def shift_step(z, carry):
        for s in range(3):
            xs[s, 1 + z] = xf[z, :, 7 + s:7 + s + ny, :].astype(BF16)
        return carry

    lax.fori_loop(0, nz, shift_step, 0)

    get_kern.wait()
    for py in range(2):
        for px in range(2):
            for c in range(2):
                row = px * ch + c * half
                for ux in range(2):
                    for vy in range(2):
                        for dz in range(3):
                            col = ((ux * 2 + vy) * 3 + dz) * ch
                            tz = TAP_Z[c][dz]
                            block = jnp.zeros((half, ch), BF16) if tz is None else kern[TAP_X[px][ux], TAP_Y[py][vy], tz]
                            wt[py, row:row + half, col:col + ch] = block

    put_wt = pltpu.make_async_copy(wt, wt_to, sems.at[2])
    put_wt.start()

    pad = im.shape[1] - total
    im[:, total:, :] = jnp.zeros((2, pad, im.shape[2]), BF16)
    dd[:, total:, :] = jnp.zeros((2, pad, dd.shape[2]), BF16)
    bias_row = jnp.concatenate([bias[...], bias[...]], axis=1)
    get_cot.wait()

    def layer_step(z, acc):
        base = pl.multiple_of(z * rows, ny)
        c32[...] = cot[:, :, z].astype(F32)
        ch32[0] = xlo[z, 0:2 * ny].astype(F32)
        ch32[1] = xhi[z, 0:2 * ny].astype(F32)
        for py in range(2):
            for ux in range(2):
                for vy in range(2):
                    for dz in range(3):
                        col = ((ux * 2 + vy) * 3 + dz) * ch
                        im[py, pl.ds(base, rows), col:col + ch] = xs[SHIFT_Y[py][vy], z + dz, ux:ux + nx + 1].reshape(rows, ch)
            pre = dot_nt(im[py, pl.ds(base, rows), :], wt[py])
            dd[py, pl.ds(base, ny), 0:ch] = jnp.zeros((ny, ch), BF16)
            dd[py, pl.ds(base + nx * ny, ny), ch:2 * ch] = jnp.zeros((ny, ch), BF16)
            for q in range(2):
                part = pre[0:nx * ny, ch:2 * ch] if q == 0 else pre[ny:, 0:ch]
                part = part + bias_row
                up = part > 0
                cots = c32[:, q, pl.ds(py, ny, stride=2), :].reshape(nx * ny, ch)
                grad = (cots * jnp.where(up, 1.0, SLOPE)).astype(BF16)
                o32[:, q, pl.ds(py, ny, stride=2), :] = jnp.where(up, part, SLOPE * part).reshape(nx, ny, ch)
                if q == 0:
                    dd[py, pl.ds(base, nx * ny), ch:2 * ch] = grad
                else:
                    dd[py, pl.ds(base + ny, nx * ny), 0:ch] = grad
                dpre[py, q:q + nx, 1 - q, z] = grad.reshape(nx, ny, ch)
                acc = acc + jnp.sum(grad.astype(F32).reshape(nx * ny // 8, 8, ch), axis=0)
            for side in range(2):
                part = (pre[0:ny, 0:ch] if side == 0 else pre[nx * ny:, ch:2 * ch]) + bias_row
                cots = ch32[side, pl.ds(py, ny, stride=2), :]
                dpre[py, side * nx, side, z] = (cots * jnp.where(part > 0, 1.0, SLOPE)).astype(BF16)
        out[:, :, z] = o32[...].astype(BF16)
        return acc

    sums = jnp.sum(lax.fori_loop(0, nz, layer_step, jnp.zeros((8, ch), F32)), axis=0, keepdims=True)
    put_out = pltpu.make_async_copy(out, out_to, sems.at[3])
    put_out.start()
    put_dpre = pltpu.make_async_copy(dpre, dpre_to, sems.at[4])
    put_dpre.start()
    high = sums.astype(BF16)
    rest = (sums - high.astype(F32)).astype(BF16)
    bgrad[...] = jnp.broadcast_to(high.astype(F32) + rest.astype(F32), bgrad.shape)

    for py in range(2):
        ddt[py] = dd[py].T
    for py in range(2):
        for block in range(im.shape[2] // (2 * ch)):
            terms = jnp.dot(ddt[py], im[py, :, block * 2 * ch:(block + 1) * 2 * ch], preferred_element_type=F32)
            for side in range(2):
                which = block * 2 + side
                ux, vy, dz = which // 6, which // 3 % 2, which % 3
                for px in range(2):
                    for c in range(2):
                        tz = TAP_Z[c][dz]
                        if tz is not None:
                            tx = TAP_X[px][ux]
                            at = (((tx % 2) * 4 + TAP_Y[py][vy]) * 4 + tz) * half
                            row = px * ch + c * half
                            kgrad[tx // 2, at:at + half] = terms[row:row + half, side * ch:(side + 1) * ch]
    mine = upper[0]
    taps = keep.shape[0]
    keep[...] = kgrad[mine]
    give[0:taps] = kgrad[1 - mine].astype(BF16)
    for k, extra in enumerate((high, rest)):
        give[taps + 8 * k:taps + 8 * k + 8] = jnp.broadcast_to(extra, (8, ch))
    put_wt.wait()
    put_out.wait()
    put_dpre.wait()


def run_forward(upper, low, ylo, yhi, xlo, xhi, kern, bias_row, cot):
    nx, nz, ny, ch = low.shape
    rows = (nx + 1) * ny
    padded = -(-rows * nz // 128) * 128
    pairs = cot.reshape(nx, 2, nz, 2 * ny, ch)
    vmem, stay = pl.BlockSpec(memory_space=pltpu.VMEM), pl.BlockSpec(memory_space=pl.ANY)
    taps = 32 * ch // 2
    out, dpre, keep, give, bgrad, wt = pl.pallas_call(
        forward_body,
        out_shape=(
            jax.ShapeDtypeStruct((nx, 2, nz, 2 * ny, ch), BF16),
            jax.ShapeDtypeStruct((2, nx + 1, 2, nz, ny, ch), BF16),
            jax.ShapeDtypeStruct((taps, ch), F32),
            jax.ShapeDtypeStruct((taps + 16, ch), BF16),
            jax.ShapeDtypeStruct((8, ch), F32),
            jax.ShapeDtypeStruct((2, 2 * ch, 12 * ch), BF16),
        ),
        in_specs=[pl.BlockSpec(memory_space=pltpu.SMEM)] + [vmem] * 5 + [stay, vmem, stay],
        out_specs=(stay, stay, vmem, vmem, vmem, stay),
        scratch_shapes=[
            pltpu.VMEM((nz, nx + 2, ny + 16, ch), F32),
            pltpu.VMEM((3, nz + 2, nx + 2, ny, ch), BF16),
            pltpu.VMEM((2, padded, 12 * ch), BF16),
            pltpu.VMEM((nx, 2, 2 * ny, ch), F32),
            pltpu.VMEM((nx, 2, 2 * ny, ch), F32),
            pltpu.VMEM((2, 2 * ny, ch), F32),
            pltpu.VMEM((2, padded, 2 * ch), BF16),
            pltpu.VMEM((2, 2 * ch, padded), BF16),
            pltpu.VMEM((2, taps, ch), F32),
            pltpu.VMEM(kern.shape, BF16),
            pltpu.VMEM(pairs.shape, BF16),
            pltpu.VMEM(pairs.shape, BF16),
            pltpu.VMEM((2, nx + 1, 2, nz, ny, ch), BF16),
            pltpu.VMEM((2, 2 * ch, 12 * ch), BF16),
            pltpu.SemaphoreType.DMA((5,)),
        ],
        compiler_params=pltpu.CompilerParams(vmem_limit_bytes=56 << 20),
        cost_estimate=pl.CostEstimate(flops=12 * 2**30, bytes_accessed=8 << 20, transcendentals=0),
        name="forward",
    )(upper, low, ylo, yhi, xlo, xhi, kern, bias_row, pairs)
    return out.reshape(2 * nx, nz, 2 * ny, ch), dpre, keep, give, bgrad, wt


def backward_body(dpre, cols, ccols, kern, bias, wt, grad, df, ds, wb, gh):
    _, duals, _, nz, ny, ch = dpre.shape
    nx = duals - 1
    half = ch // 2
    lanes = gh.shape[3]
    bias_row = jnp.concatenate([bias[...], bias[...]], axis=1)
    for py in range(2):
        pieces = []
        for ux in range(2):
            for vy in range(2):
                which = ((3, 2), (0, 1))[py][vy]
                for dz in range(3):
                    pieces.append(cols[which, dz:dz + nz, ux:ux + lanes, :].reshape(nz * lanes, ch).astype(BF16))
        pre = dot_nt(jnp.concatenate(pieces, axis=1), wt[py])
        for px in range(2):
            part = pre[:, px * ch:(px + 1) * ch] + bias_row
            cots = ccols[py, px].reshape(nz * lanes, ch)
            gh[py, px] = (cots * jnp.where(part > 0, 1.0, SLOPE)).astype(BF16).astype(F32).reshape(nz, lanes, ch)
    zero = jnp.zeros((nx + 1, 2, ny, ch), BF16)
    for var in range(4):
        ds[var, 0] = zero
        ds[var, nz + 1] = zero

    def layer_load(z, carry):
        for py in range(2):
            df[py, :, :, 8:8 + ny, :] = dpre[py, :, :, z].astype(F32)
            for px in range(2):
                df[py, :, px, 7 if py else 8 + ny, :] = gh[py, px, z, 0:nx + 1]
        for py in range(2):
            for vy in range(2):
                lead = 8 if vy == 0 else (9 if py == 0 else 7)
                ds[py * 2 + vy, 1 + z] = df[py, :, :, lead:lead + ny, :].astype(BF16)
        return carry

    lax.fori_loop(0, nz, layer_load, 0)
    for py in range(2):
        for vy in range(2):
            for q in range(4):
                row = ((py * 2 + vy) * 4 + q) * 2 * ch
                ty = TAP_Y[py][vy]
                for place, tz in enumerate((1, 2, 3, 0)):
                    at = row + place * half
                    wb[at:at + half, :] = kern[q, ty, tz]
    lane = lax.broadcasted_iota(jnp.int32, (nx, ny, ch), 2)

    def layer_step(z, carry):
        acc = jnp.zeros((nx * ny, ch), F32)
        for var in range(4):
            pieces = []
            for q in range(4):
                same = ds[var, 1 + z, q // 2:q // 2 + nx, q % 2]
                above = ds[var, 2 + z, q // 2:q // 2 + nx, q % 2]
                below = ds[var, z, q // 2:q // 2 + nx, q % 2]
                mixed = jnp.where(lane < half, above.astype(F32), below.astype(F32)).astype(BF16)
                pieces += [same.reshape(nx * ny, ch), mixed.reshape(nx * ny, ch)]
            acc = acc + jnp.dot(jnp.concatenate(pieces, axis=1), wb[var * 8 * ch:(var + 1) * 8 * ch, :], preferred_element_type=F32)
        grad[:, z] = acc.astype(BF16).reshape(nx, ny, ch)
        return carry

    lax.fori_loop(0, nz, layer_step, 0)


def run_backward(dpre, cols, ccols, kern, bias_row, wt):
    _, duals, _, nz, ny, ch = dpre.shape
    nx = duals - 1
    vmem = pl.BlockSpec(memory_space=pltpu.VMEM)
    return pl.pallas_call(
        backward_body,
        out_shape=jax.ShapeDtypeStruct((nx, nz, ny, ch), BF16),
        in_specs=[vmem] * 6,
        out_specs=vmem,
        scratch_shapes=[
            pltpu.VMEM((2, nx + 1, 2, ny + 16, ch), F32),
            pltpu.VMEM((4, nz + 2, nx + 1, 2, ny, ch), BF16),
            pltpu.VMEM((32 * ch, ch), BF16),
            pltpu.VMEM((2, 2, nz, nx + 8, ch), F32),
        ],
        compiler_params=pltpu.CompilerParams(vmem_limit_bytes=40 << 20),
        cost_estimate=pl.CostEstimate(flops=4 * 2**30, bytes_accessed=4 << 20, transcendentals=0),
        name="backward",
    )(dpre, cols, ccols, kern, bias_row, wt)


def from_both(first, last, axis):
    count = lax.axis_size(axis)
    odd = lax.axis_index(axis) % 2 == 1
    inner = lax.ppermute(jnp.where(odd, first, last), axis, [(i, i ^ 1) for i in range(count)])
    outer = lax.ppermute(jnp.where(odd, last, first), axis, [(i, i + 1 if i % 2 else i - 1) for i in range(1, count - 1)])
    return jnp.where(odd, inner, outer), jnp.where(odd, outer, inner)


HALVE = (("gy", 1), ("gy", 4), ("gy", 2), ("gy", 8))
GROUPS = (("gx", (1, 8, 9)), ("gx", (2, 5, 7)))


def swap(values, axis, bits):
    return lax.ppermute(values, axis, [(i, i ^ bits) for i in range(lax.axis_size(axis))])


def rounded(values):
    return lax.reduce_precision(values, 8, 7)


def with_extra(values, extra):
    high = rounded(extra)
    tail = [jnp.broadcast_to(part.astype(BF16), (8,) + part.shape[1:]) for part in (high, rounded(extra - high))]
    return jnp.concatenate([values.astype(BF16)] + tail, axis=0), high + rounded(extra - high)


def take_extra(message):
    rows = message.shape[0] - 16
    wide = message.astype(F32)
    return wide[:rows], wide[rows:rows + 1] + wide[rows + 8:rows + 9]


def sum_over_devices(keep, message, brow):
    steps = [(axis, bit) for axis, bit in HALVE if bit < lax.axis_size(axis)]
    groups = [(axis, [bits for bits in some if bits < lax.axis_size(axis)]) for axis, some in GROUPS]
    extra = brow[0:1]
    for at, (axis, bit) in enumerate(steps):
        if at:
            half = part.shape[0] // 2
            up = (lax.axis_index(axis) & bit) != 0
            keep = jnp.where(up, part[half:], part[:half])
            message, extra = with_extra(jnp.where(up, part[:half], part[half:]), extra)
        came, came_extra = take_extra(swap(message, axis, bit))
        part = keep + came
        extra = extra + came_extra
    for axis, some in groups:
        own = rounded(part)
        message, own_extra = with_extra(own, extra)
        arrived = [take_extra(swap(message, axis, bits)) for bits in some]
        if len(arrived) == 3:
            part = (own + arrived[0][0]) + (arrived[1][0] + arrived[2][0])
            extra = (own_extra + arrived[0][1]) + (arrived[1][1] + arrived[2][1])
        else:
            for more, more_extra in arrived:
                part, extra = own + more, own_extra + more_extra
    grown = part.astype(BF16)
    for axis, bit in steps[::-1]:
        up = (lax.axis_index(axis) & bit) != 0
        came = swap(grown, axis, bit)
        grown = jnp.concatenate([jnp.where(up, came, grown), jnp.where(up, grown, came)], axis=0)
    return grown.astype(F32), extra


def per_device(low_res, kernel, bias, cotangent):
    low = jnp.transpose(low_res, (0, 2, 1, 3))
    cot = jnp.transpose(cotangent, (0, 2, 1, 3))
    nx, nz, ny, ch = low.shape
    bias_row = bias.reshape(1, -1)

    first = jnp.concatenate([low[:, :, 0], cot[:, :, 0]], axis=0)
    last = jnp.concatenate([low[:, :, ny - 1], cot[:, :, 2 * ny - 1]], axis=0)
    ylo, yhi = from_both(first, last, "gy")

    def row(cell, output):
        pieces = [cot[output], ylo[cell][:, None], low[cell], yhi[cell][:, None], ylo[nx + output][:, None], yhi[nx + output][:, None]]
        return jnp.concatenate(pieces, axis=1)

    xlo, xhi = from_both(row(0, 0), row(nx - 1, 2 * nx - 1), "gx")
    axis, bit = HALVE[0]
    upper = (lax.axis_index(axis) // bit % 2).astype(jnp.int32).reshape(1)
    out, dpre, keep, give, bgrad, wt = run_forward(upper, low, ylo, yhi, xlo, xhi, kernel, bias_row, cot)

    def column(at, middle):
        first, last = xlo[:, at][:, None], xhi[:, at][:, None]
        return jnp.concatenate([first, jnp.transpose(middle, (1, 0, 2)), last], axis=1)

    cols = jnp.stack([column(2 * ny, ylo[:nx]), column(2 * ny + 1, low[:, :, 0]), column(3 * ny, low[:, :, ny - 1]), column(3 * ny + 1, yhi[:nx])])
    cols = jnp.pad(cols.astype(F32), ((0, 0), (1, 1), (0, 14), (0, 0)))
    ccols = jnp.stack([column(3 * ny + 3, yhi[nx:]), column(3 * ny + 2, ylo[nx:])]).astype(F32)
    ccols = jnp.transpose(ccols.reshape(2, nz, nx + 1, 2, ch), (0, 3, 1, 2, 4))
    ccols = jnp.pad(ccols, ((0, 0), (0, 0), (0, 0), (0, 7), (0, 0)))
    grad = run_backward(dpre, cols, ccols, kernel, bias_row, wt)
    kernel_sum, bias_sum = sum_over_devices(keep, give, bgrad)

    grid_rows = lax.axis_size("gx") * nx
    output = jnp.transpose(out, (0, 2, 1, 3))
    input_grad = jnp.transpose(grad, (0, 2, 1, 3))
    kernel_grad = kernel_sum.reshape(kernel.shape) / grid_rows
    bias_grad = jnp.sum(bias_sum.reshape(2, ch // 2), axis=0) / grid_rows
    return (output, input_grad, kernel_grad, bias_grad)


def solution(mesh):
    return jax.shard_map(
        per_device,
        mesh=mesh,
        in_specs=(P("gx", "gy", None, None), P(), P(), P("gx", "gy", None, None)),
        out_specs=(P("gx", "gy", None, None), P("gx", "gy", None, None), P(), P()),
        check_vma=False,
    )
```

```python
import jax
import jax.numpy as jnp
from jax import lax
from jax.experimental import pallas as pl
from jax.experimental.pallas import tpu as pltpu
from jax.sharding import PartitionSpec as P


SLOPE = 0.2
F32 = jnp.float32
BF16 = jnp.bfloat16

TAP_X = ((2, 0), (3, 1))
TAP_Y = ((1, 3), (2, 0))
SHIFT_Y = ((1, 0), (1, 2))
TAP_Z = ((3, 1, None), (None, 2, 0))


def dot_nt(a, b):
    return lax.dot_general(a, b, (((1,), (1,)), ((), ())), preferred_element_type=F32)


def build_weights(kern, wt):
    half, ch = kern.shape[3:]
    for py in range(2):
        for px in range(2):
            for c in range(2):
                row = px * ch + c * half
                for ux in range(2):
                    for vy in range(2):
                        for dz in range(3):
                            col = ((ux * 2 + vy) * 3 + dz) * ch
                            tz = TAP_Z[c][dz]
                            block = jnp.zeros((half, ch), BF16) if tz is None else kern[TAP_X[px][ux], TAP_Y[py][vy], tz]
                            wt[py, row:row + half, col:col + ch] = block


def forward_body(upper, low, ylo, yhi, xlo, xhi, kern_in, bias, cot_in, out_to, dpre_to, keep, give, bgrad, xf, xs, im, c32, o32, ch32, dd, ddt, kgrad, kern, cot, out, dpre, wt, sems):
    get_kern = pltpu.make_async_copy(kern_in, kern, sems.at[0])
    get_kern.start()
    get_cot = pltpu.make_async_copy(cot_in, cot, sems.at[1])
    get_cot.start()
    nx, nz, ny, ch = low.shape
    half = ch // 2
    rows = (nx + 1) * ny
    total = rows * nz

    for z in range(nz):
        xf[z, pl.ds(1, nx), 8:8 + ny, :] = low[:, z].astype(F32)
        xf[z, 0, 7:9 + ny, :] = xlo[z, 2 * ny:3 * ny + 2].astype(F32)
        xf[z, nx + 1, 7:9 + ny, :] = xhi[z, 2 * ny:3 * ny + 2].astype(F32)
    for x in range(nx):
        xf[:, 1 + x, 7, :] = ylo[x].astype(F32)
        xf[:, 1 + x, 8 + ny, :] = yhi[x].astype(F32)
    xs[:, 0] = jnp.zeros(xs.shape[:1] + xs.shape[2:], BF16)
    xs[:, nz + 1] = jnp.zeros(xs.shape[:1] + xs.shape[2:], BF16)

    def shift_step(z, carry):
        for s in range(3):
            xs[s, 1 + z] = xf[z, :, 7 + s:7 + s + ny, :].astype(BF16)
        return carry

    lax.fori_loop(0, nz, shift_step, 0)

    get_kern.wait()
    build_weights(kern, wt)

    pad = im.shape[1] - total
    im[:, total:, :] = jnp.zeros((2, pad, im.shape[2]), BF16)
    dd[:, total:, :] = jnp.zeros((2, pad, dd.shape[2]), BF16)
    bias_row = jnp.concatenate([bias[...], bias[...]], axis=1)
    get_cot.wait()

    def layer_step(z, acc):
        base = pl.multiple_of(z * rows, ny)
        c32[...] = cot[:, :, z].astype(F32)
        ch32[0] = xlo[z, 0:2 * ny].astype(F32)
        ch32[1] = xhi[z, 0:2 * ny].astype(F32)
        for py in range(2):
            for ux in range(2):
                for vy in range(2):
                    for dz in range(3):
                        col = ((ux * 2 + vy) * 3 + dz) * ch
                        im[py, pl.ds(base, rows), col:col + ch] = xs[SHIFT_Y[py][vy], z + dz, ux:ux + nx + 1].reshape(rows, ch)
            pre = dot_nt(im[py, pl.ds(base, rows), :], wt[py])
            dd[py, pl.ds(base, ny), 0:ch] = jnp.zeros((ny, ch), BF16)
            dd[py, pl.ds(base + nx * ny, ny), ch:2 * ch] = jnp.zeros((ny, ch), BF16)
            for q in range(2):
                part = pre[0:nx * ny, ch:2 * ch] if q == 0 else pre[ny:, 0:ch]
                part = part + bias_row
                up = part > 0
                cots = c32[:, q, pl.ds(py, ny, stride=2), :].reshape(nx * ny, ch)
                grad = (cots * jnp.where(up, 1.0, SLOPE)).astype(BF16)
                o32[:, q, pl.ds(py, ny, stride=2), :] = jnp.where(up, part, SLOPE * part).reshape(nx, ny, ch)
                if q == 0:
                    dd[py, pl.ds(base, nx * ny), ch:2 * ch] = grad
                else:
                    dd[py, pl.ds(base + ny, nx * ny), 0:ch] = grad
                dpre[py, q:q + nx, 1 - q, z] = grad.reshape(nx, ny, ch)
                acc = acc + jnp.sum(grad.astype(F32).reshape(nx * ny // 8, 8, ch), axis=0)
            for side in range(2):
                part = (pre[0:ny, 0:ch] if side == 0 else pre[nx * ny:, ch:2 * ch]) + bias_row
                cots = ch32[side, pl.ds(py, ny, stride=2), :]
                dpre[py, side * nx, side, z] = (cots * jnp.where(part > 0, 1.0, SLOPE)).astype(BF16)
        out[:, :, z] = o32[...].astype(BF16)
        return acc

    sums = jnp.sum(lax.fori_loop(0, nz, layer_step, jnp.zeros((8, ch), F32)), axis=0, keepdims=True)
    put_out = pltpu.make_async_copy(out, out_to, sems.at[3])
    put_out.start()
    put_dpre = pltpu.make_async_copy(dpre, dpre_to, sems.at[4])
    put_dpre.start()
    high = sums.astype(BF16)
    rest = (sums - high.astype(F32)).astype(BF16)
    bgrad[...] = jnp.broadcast_to(high.astype(F32) + rest.astype(F32), bgrad.shape)

    for py in range(2):
        ddt[py] = dd[py].T
    for py in range(2):
        for block in range(im.shape[2] // (2 * ch)):
            terms = jnp.dot(ddt[py], im[py, :, block * 2 * ch:(block + 1) * 2 * ch], preferred_element_type=F32)
            for side in range(2):
                which = block * 2 + side
                ux, vy, dz = which // 6, which // 3 % 2, which % 3
                for px in range(2):
                    for c in range(2):
                        tz = TAP_Z[c][dz]
                        if tz is not None:
                            tx = TAP_X[px][ux]
                            at = (((tx % 2) * 4 + TAP_Y[py][vy]) * 4 + tz) * half
                            row = px * ch + c * half
                            kgrad[tx // 2, at:at + half] = terms[row:row + half, side * ch:(side + 1) * ch]
    mine = upper[0]
    taps = keep.shape[0]
    keep[...] = kgrad[mine]
    give[0:taps] = kgrad[1 - mine].astype(BF16)
    for k, extra in enumerate((high, rest)):
        give[taps + 8 * k:taps + 8 * k + 8] = jnp.broadcast_to(extra, (8, ch))
    put_out.wait()
    put_dpre.wait()


def run_forward(upper, low, ylo, yhi, xlo, xhi, kern, bias_row, cot):
    nx, nz, ny, ch = low.shape
    rows = (nx + 1) * ny
    padded = -(-rows * nz // 128) * 128
    pairs = cot.reshape(nx, 2, nz, 2 * ny, ch)
    vmem, stay = pl.BlockSpec(memory_space=pltpu.VMEM), pl.BlockSpec(memory_space=pl.ANY)
    taps = 32 * ch // 2
    out, dpre, keep, give, bgrad = pl.pallas_call(
        forward_body,
        out_shape=(
            jax.ShapeDtypeStruct((nx, 2, nz, 2 * ny, ch), BF16),
            jax.ShapeDtypeStruct((2, nx + 1, 2, nz, ny, ch), BF16),
            jax.ShapeDtypeStruct((taps, ch), F32),
            jax.ShapeDtypeStruct((taps + 16, ch), BF16),
            jax.ShapeDtypeStruct((8, ch), F32),
        ),
        in_specs=[pl.BlockSpec(memory_space=pltpu.SMEM)] + [vmem] * 5 + [stay, vmem, stay],
        out_specs=(stay, stay, vmem, vmem, vmem),
        scratch_shapes=[
            pltpu.VMEM((nz, nx + 2, ny + 16, ch), F32),
            pltpu.VMEM((3, nz + 2, nx + 2, ny, ch), BF16),
            pltpu.VMEM((2, padded, 12 * ch), BF16),
            pltpu.VMEM((nx, 2, 2 * ny, ch), F32),
            pltpu.VMEM((nx, 2, 2 * ny, ch), F32),
            pltpu.VMEM((2, 2 * ny, ch), F32),
            pltpu.VMEM((2, padded, 2 * ch), BF16),
            pltpu.VMEM((2, 2 * ch, padded), BF16),
            pltpu.VMEM((2, taps, ch), F32),
            pltpu.VMEM(kern.shape, BF16),
            pltpu.VMEM(pairs.shape, BF16),
            pltpu.VMEM(pairs.shape, BF16),
            pltpu.VMEM((2, nx + 1, 2, nz, ny, ch), BF16),
            pltpu.VMEM((2, 2 * ch, 12 * ch), BF16),
            pltpu.SemaphoreType.DMA((5,)),
        ],
        compiler_params=pltpu.CompilerParams(vmem_limit_bytes=56 << 20),
        cost_estimate=pl.CostEstimate(flops=12 * 2**30, bytes_accessed=8 << 20, transcendentals=0),
        name="forward",
    )(upper, low, ylo, yhi, xlo, xhi, kern, bias_row, pairs)
    return out.reshape(2 * nx, nz, 2 * ny, ch), dpre, keep, give, bgrad


def backward_body(dpre, cols, ccols, kern, bias, grad, df, ds, wb, gh, wt):
    build_weights(kern, wt)
    _, duals, _, nz, ny, ch = dpre.shape
    nx = duals - 1
    half = ch // 2
    lanes = gh.shape[3]
    bias_row = jnp.concatenate([bias[...], bias[...]], axis=1)
    for py in range(2):
        pieces = []
        for ux in range(2):
            for vy in range(2):
                which = ((3, 2), (0, 1))[py][vy]
                for dz in range(3):
                    pieces.append(cols[which, dz:dz + nz, ux:ux + lanes, :].reshape(nz * lanes, ch).astype(BF16))
        pre = dot_nt(jnp.concatenate(pieces, axis=1), wt[py])
        for px in range(2):
            part = pre[:, px * ch:(px + 1) * ch] + bias_row
            cots = ccols[py, px].reshape(nz * lanes, ch)
            gh[py, px] = (cots * jnp.where(part > 0, 1.0, SLOPE)).astype(BF16).astype(F32).reshape(nz, lanes, ch)
    zero = jnp.zeros((nx + 1, 2, ny, ch), BF16)
    for var in range(4):
        ds[var, 0] = zero
        ds[var, nz + 1] = zero

    def layer_load(z, carry):
        for py in range(2):
            df[py, :, :, 8:8 + ny, :] = dpre[py, :, :, z].astype(F32)
            for px in range(2):
                df[py, :, px, 7 if py else 8 + ny, :] = gh[py, px, z, 0:nx + 1]
        for py in range(2):
            for vy in range(2):
                lead = 8 if vy == 0 else (9 if py == 0 else 7)
                ds[py * 2 + vy, 1 + z] = df[py, :, :, lead:lead + ny, :].astype(BF16)
        return carry

    lax.fori_loop(0, nz, layer_load, 0)
    for py in range(2):
        for vy in range(2):
            for q in range(4):
                row = ((py * 2 + vy) * 4 + q) * 2 * ch
                ty = TAP_Y[py][vy]
                for place, tz in enumerate((1, 2, 3, 0)):
                    at = row + place * half
                    wb[at:at + half, :] = kern[q, ty, tz]
    lane = lax.broadcasted_iota(jnp.int32, (nx, ny, ch), 2)

    def layer_step(z, carry):
        acc = jnp.zeros((nx * ny, ch), F32)
        for var in range(4):
            pieces = []
            for q in range(4):
                same = ds[var, 1 + z, q // 2:q // 2 + nx, q % 2]
                above = ds[var, 2 + z, q // 2:q // 2 + nx, q % 2]
                below = ds[var, z, q // 2:q // 2 + nx, q % 2]
                mixed = jnp.where(lane < half, above.astype(F32), below.astype(F32)).astype(BF16)
                pieces += [same.reshape(nx * ny, ch), mixed.reshape(nx * ny, ch)]
            acc = acc + jnp.dot(jnp.concatenate(pieces, axis=1), wb[var * 8 * ch:(var + 1) * 8 * ch, :], preferred_element_type=F32)
        grad[:, z] = acc.astype(BF16).reshape(nx, ny, ch)
        return carry

    lax.fori_loop(0, nz, layer_step, 0)


def run_backward(dpre, cols, ccols, kern, bias_row):
    _, duals, _, nz, ny, ch = dpre.shape
    nx = duals - 1
    vmem = pl.BlockSpec(memory_space=pltpu.VMEM)
    return pl.pallas_call(
        backward_body,
        out_shape=jax.ShapeDtypeStruct((nx, nz, ny, ch), BF16),
        in_specs=[vmem] * 5,
        out_specs=vmem,
        scratch_shapes=[
            pltpu.VMEM((2, nx + 1, 2, ny + 16, ch), F32),
            pltpu.VMEM((4, nz + 2, nx + 1, 2, ny, ch), BF16),
            pltpu.VMEM((32 * ch, ch), BF16),
            pltpu.VMEM((2, 2, nz, nx + 8, ch), F32),
            pltpu.VMEM((2, 2 * ch, 12 * ch), BF16),
        ],
        compiler_params=pltpu.CompilerParams(vmem_limit_bytes=40 << 20),
        cost_estimate=pl.CostEstimate(flops=4 * 2**30, bytes_accessed=4 << 20, transcendentals=0),
        name="backward",
    )(dpre, cols, ccols, kern, bias_row)


def from_both(first, last, axis):
    count = lax.axis_size(axis)
    odd = lax.axis_index(axis) % 2 == 1
    inner = lax.ppermute(jnp.where(odd, first, last), axis, [(i, i ^ 1) for i in range(count)])
    other = jnp.where(odd, last, first)
    outer = lax.ppermute(other, axis, [(i, i + 1 if i % 2 else i - 1) for i in range(1, count - 1)])
    return jnp.where(odd, inner, outer), jnp.where(odd, outer, inner)


HALVE = (("gy", 1), ("gy", 4), ("gy", 2), ("gy", 8))
GROUPS = (("gx", (1, 8, 9)), ("gx", (2, 5, 7)))


def swap(values, axis, bits):
    return lax.ppermute(values, axis, [(i, i ^ bits) for i in range(lax.axis_size(axis))])


def rounded(values):
    return lax.reduce_precision(values, 8, 7)


def with_extra(values, extra):
    high = rounded(extra)
    tail = [jnp.broadcast_to(part.astype(BF16), (8,) + part.shape[1:]) for part in (high, rounded(extra - high))]
    return jnp.concatenate([values.astype(BF16)] + tail, axis=0), high + rounded(extra - high)


def take_extra(message):
    rows = message.shape[0] - 16
    wide = message.astype(F32)
    return wide[:rows], wide[rows:rows + 1] + wide[rows + 8:rows + 9]


def sum_over_devices(keep, message, brow):
    steps = [(axis, bit) for axis, bit in HALVE if bit < lax.axis_size(axis)]
    groups = [(axis, [bits for bits in some if bits < lax.axis_size(axis)]) for axis, some in GROUPS]
    extra = brow[0:1]
    for at, (axis, bit) in enumerate(steps):
        if at:
            half = part.shape[0] // 2
            up = (lax.axis_index(axis) & bit) != 0
            keep = jnp.where(up, part[half:], part[:half])
            message, extra = with_extra(jnp.where(up, part[:half], part[half:]), extra)
        came, came_extra = take_extra(swap(message, axis, bit))
        part = keep + came
        extra = extra + came_extra
    for axis, some in groups:
        own = rounded(part)
        message, own_extra = with_extra(own, extra)
        arrived = [take_extra(swap(message, axis, bits)) for bits in some]
        if len(arrived) == 3:
            part = (own + arrived[0][0]) + (arrived[1][0] + arrived[2][0])
            extra = (own_extra + arrived[0][1]) + (arrived[1][1] + arrived[2][1])
        else:
            for more, more_extra in arrived:
                part, extra = own + more, own_extra + more_extra
    grown = part.astype(BF16)
    for axis, bit in steps[::-1]:
        up = (lax.axis_index(axis) & bit) != 0
        came = swap(grown, axis, bit)
        grown = jnp.concatenate([jnp.where(up, came, grown), jnp.where(up, grown, came)], axis=0)
    return grown.astype(F32), extra


def per_device(low_res, kernel, bias, cotangent):
    low = jnp.transpose(low_res, (0, 2, 1, 3))
    cot = jnp.transpose(cotangent, (0, 2, 1, 3))
    nx, nz, ny, ch = low.shape
    bias_row = bias.reshape(1, -1)

    first = jnp.concatenate([low[:, :, 0], cot[:, :, 0]], axis=0)
    last = jnp.concatenate([low[:, :, ny - 1], cot[:, :, 2 * ny - 1]], axis=0)
    ylo, yhi = from_both(first, last, "gy")

    def row(cell, output):
        pieces = [cot[output], ylo[cell][:, None], low[cell], yhi[cell][:, None], ylo[nx + output][:, None], yhi[nx + output][:, None]]
        return jnp.concatenate(pieces, axis=1)

    xlo, xhi = from_both(row(0, 0), row(nx - 1, 2 * nx - 1), "gx")
    axis, bit = HALVE[0]
    upper = (lax.axis_index(axis) // bit % 2).astype(jnp.int32).reshape(1)
    out, dpre, keep, give, bgrad = run_forward(upper, low, ylo, yhi, xlo, xhi, kernel, bias_row, cot)

    def column(at, middle):
        first, last = xlo[:, at][:, None], xhi[:, at][:, None]
        return jnp.concatenate([first, jnp.transpose(middle, (1, 0, 2)), last], axis=1)

    cols = jnp.stack([column(2 * ny, ylo[:nx]), column(2 * ny + 1, low[:, :, 0]), column(3 * ny, low[:, :, ny - 1]), column(3 * ny + 1, yhi[:nx])])
    cols = jnp.pad(cols.astype(F32), ((0, 0), (1, 1), (0, 14), (0, 0)))
    ccols = jnp.stack([column(3 * ny + 3, yhi[nx:]), column(3 * ny + 2, ylo[nx:])]).astype(F32)
    ccols = jnp.transpose(ccols.reshape(2, nz, nx + 1, 2, ch), (0, 3, 1, 2, 4))
    ccols = jnp.pad(ccols, ((0, 0), (0, 0), (0, 0), (0, 7), (0, 0)))
    grad = run_backward(dpre, cols, ccols, kernel, bias_row)
    kernel_sum, bias_sum = sum_over_devices(keep, give, bgrad)

    grid_rows = lax.axis_size("gx") * nx
    output = jnp.transpose(out, (0, 2, 1, 3))
    input_grad = jnp.transpose(grad, (0, 2, 1, 3))
    kernel_grad = kernel_sum.reshape(kernel.shape) / grid_rows
    bias_grad = jnp.sum(bias_sum.reshape(2, ch // 2), axis=0) / grid_rows
    return (output, input_grad, kernel_grad, bias_grad)


def solution(mesh):
    return jax.shard_map(
        per_device,
        mesh=mesh,
        in_specs=(P("gx", "gy", None, None), P(), P(), P("gx", "gy", None, None)),
        out_specs=(P("gx", "gy", None, None), P("gx", "gy", None, None), P(), P()),
        check_vma=False,
    )
```

```python
import jax
import jax.numpy as jnp
from jax import lax
from jax.experimental import pallas as pl
from jax.experimental.pallas import tpu as pltpu
from jax.sharding import PartitionSpec as P


SLOPE = 0.2
F32 = jnp.float32
BF16 = jnp.bfloat16

TAP_X = ((2, 0), (3, 1))
TAP_Y = ((1, 3), (2, 0))
SHIFT_Y = ((1, 0), (1, 2))
TAP_Z = ((3, 1, None), (None, 2, 0))


def dot_nt(a, b):
    return lax.dot_general(a, b, (((1,), (1,)), ((), ())), preferred_element_type=F32)


def build_weights(kern, wt):
    half, ch = kern.shape[3:]
    for py in range(2):
        for px in range(2):
            for c in range(2):
                row = px * ch + c * half
                for ux in range(2):
                    for vy in range(2):
                        for dz in range(3):
                            col = ((ux * 2 + vy) * 3 + dz) * ch
                            tz = TAP_Z[c][dz]
                            block = jnp.zeros((half, ch), BF16) if tz is None else kern[TAP_X[px][ux], TAP_Y[py][vy], tz]
                            wt[py, row:row + half, col:col + ch] = block


def forward_body(upper, low, ylo, yhi, xlo, xhi, kern_in, bias, cot_in, out_to, dpre_to, keep, give, bgrad, xf, xs, im, c32, o32, ch32, dd, ddt, kgrad, kern, cot, out, dpre, wt, sems):
    get_kern = pltpu.make_async_copy(kern_in, kern, sems.at[0])
    get_kern.start()
    get_cot = pltpu.make_async_copy(cot_in, cot, sems.at[1])
    get_cot.start()
    nx, nz, ny, ch = low.shape
    half = ch // 2
    rows = (nx + 1) * ny
    total = rows * nz

    for z in range(nz):
        xf[z, pl.ds(1, nx), 8:8 + ny, :] = low[:, z].astype(F32)
        xf[z, 0, 7:9 + ny, :] = xlo[z, 2 * ny:3 * ny + 2].astype(F32)
        xf[z, nx + 1, 7:9 + ny, :] = xhi[z, 2 * ny:3 * ny + 2].astype(F32)
    for x in range(nx):
        xf[:, 1 + x, 7, :] = ylo[x].astype(F32)
        xf[:, 1 + x, 8 + ny, :] = yhi[x].astype(F32)
    xs[:, 0] = jnp.zeros(xs.shape[:1] + xs.shape[2:], BF16)
    xs[:, nz + 1] = jnp.zeros(xs.shape[:1] + xs.shape[2:], BF16)

    def shift_step(z, carry):
        for s in range(3):
            xs[s, 1 + z] = xf[z, :, 7 + s:7 + s + ny, :].astype(BF16)
        return carry

    lax.fori_loop(0, nz, shift_step, 0)

    get_kern.wait()
    build_weights(kern, wt)

    pad = im.shape[1] - total
    im[:, total:, :] = jnp.zeros((2, pad, im.shape[2]), BF16)
    dd[:, total:, :] = jnp.zeros((2, pad, dd.shape[2]), BF16)
    bias_row = jnp.concatenate([bias[...], bias[...]], axis=1)
    get_cot.wait()

    def layer_step(z, acc):
        base = pl.multiple_of(z * rows, ny)
        c32[...] = cot[:, :, z].astype(F32)
        ch32[0] = xlo[z, 0:2 * ny].astype(F32)
        ch32[1] = xhi[z, 0:2 * ny].astype(F32)
        for py in range(2):
            for ux in range(2):
                for vy in range(2):
                    for dz in range(3):
                        col = ((ux * 2 + vy) * 3 + dz) * ch
                        im[py, pl.ds(base, rows), col:col + ch] = xs[SHIFT_Y[py][vy], z + dz, ux:ux + nx + 1].reshape(rows, ch)
        both = [dot_nt(im[py, pl.ds(base, rows), :], wt[py]) for py in range(2)]
        for py in range(2):
            pre = both[py]
            dd[py, pl.ds(base, ny), 0:ch] = jnp.zeros((ny, ch), BF16)
            dd[py, pl.ds(base + nx * ny, ny), ch:2 * ch] = jnp.zeros((ny, ch), BF16)
            for q in range(2):
                part = pre[0:nx * ny, ch:2 * ch] if q == 0 else pre[ny:, 0:ch]
                part = part + bias_row
                up = part > 0
                cots = c32[:, q, pl.ds(py, ny, stride=2), :].reshape(nx * ny, ch)
                grad = (cots * jnp.where(up, 1.0, SLOPE)).astype(BF16)
                o32[:, q, pl.ds(py, ny, stride=2), :] = jnp.where(up, part, SLOPE * part).reshape(nx, ny, ch)
                if q == 0:
                    dd[py, pl.ds(base, nx * ny), ch:2 * ch] = grad
                else:
                    dd[py, pl.ds(base + ny, nx * ny), 0:ch] = grad
                dpre[py, q:q + nx, 1 - q, z] = grad.reshape(nx, ny, ch)
                acc = acc + jnp.sum(grad.astype(F32).reshape(nx * ny // 8, 8, ch), axis=0)
            for side in range(2):
                part = (pre[0:ny, 0:ch] if side == 0 else pre[nx * ny:, ch:2 * ch]) + bias_row
                cots = ch32[side, pl.ds(py, ny, stride=2), :]
                dpre[py, side * nx, side, z] = (cots * jnp.where(part > 0, 1.0, SLOPE)).astype(BF16)
        out[:, :, z] = o32[...].astype(BF16)
        return acc

    sums = jnp.sum(lax.fori_loop(0, nz, layer_step, jnp.zeros((8, ch), F32), unroll=True), axis=0, keepdims=True)
    put_out = pltpu.make_async_copy(out, out_to, sems.at[3])
    put_out.start()
    put_dpre = pltpu.make_async_copy(dpre, dpre_to, sems.at[4])
    put_dpre.start()
    high = sums.astype(BF16)
    rest = (sums - high.astype(F32)).astype(BF16)
    bgrad[...] = jnp.broadcast_to(high.astype(F32) + rest.astype(F32), bgrad.shape)

    for py in range(2):
        ddt[py] = dd[py].T
    for py in range(2):
        for block in range(im.shape[2] // (2 * ch)):
            terms = jnp.dot(ddt[py], im[py, :, block * 2 * ch:(block + 1) * 2 * ch], preferred_element_type=F32)
            for side in range(2):
                which = block * 2 + side
                ux, vy, dz = which // 6, which // 3 % 2, which % 3
                for px in range(2):
                    for c in range(2):
                        tz = TAP_Z[c][dz]
                        if tz is not None:
                            tx = TAP_X[px][ux]
                            at = (((tx % 2) * 4 + TAP_Y[py][vy]) * 4 + tz) * half
                            row = px * ch + c * half
                            kgrad[tx // 2, at:at + half] = terms[row:row + half, side * ch:(side + 1) * ch]
    mine = upper[0]
    taps = keep.shape[0]
    keep[...] = kgrad[mine]
    give[0:taps] = kgrad[1 - mine].astype(BF16)
    for k, extra in enumerate((high, rest)):
        give[taps + 8 * k:taps + 8 * k + 8] = jnp.broadcast_to(extra, (8, ch))
    put_out.wait()
    put_dpre.wait()


def run_forward(upper, low, ylo, yhi, xlo, xhi, kern, bias_row, cot):
    nx, nz, ny, ch = low.shape
    rows = (nx + 1) * ny
    padded = -(-rows * nz // 128) * 128
    pairs = cot.reshape(nx, 2, nz, 2 * ny, ch)
    vmem, stay = pl.BlockSpec(memory_space=pltpu.VMEM), pl.BlockSpec(memory_space=pl.ANY)
    taps = 32 * ch // 2
    out, dpre, keep, give, bgrad = pl.pallas_call(
        forward_body,
        out_shape=(
            jax.ShapeDtypeStruct((nx, 2, nz, 2 * ny, ch), BF16),
            jax.ShapeDtypeStruct((2, nx + 1, 2, nz, ny, ch), BF16),
            jax.ShapeDtypeStruct((taps, ch), F32),
            jax.ShapeDtypeStruct((taps + 16, ch), BF16),
            jax.ShapeDtypeStruct((8, ch), F32),
        ),
        in_specs=[pl.BlockSpec(memory_space=pltpu.SMEM)] + [vmem] * 5 + [stay, vmem, stay],
        out_specs=(stay, stay, vmem, vmem, vmem),
        scratch_shapes=[
            pltpu.VMEM((nz, nx + 2, ny + 16, ch), F32),
            pltpu.VMEM((3, nz + 2, nx + 2, ny, ch), BF16),
            pltpu.VMEM((2, padded, 12 * ch), BF16),
            pltpu.VMEM((nx, 2, 2 * ny, ch), F32),
            pltpu.VMEM((nx, 2, 2 * ny, ch), F32),
            pltpu.VMEM((2, 2 * ny, ch), F32),
            pltpu.VMEM((2, padded, 2 * ch), BF16),
            pltpu.VMEM((2, 2 * ch, padded), BF16),
            pltpu.VMEM((2, taps, ch), F32),
            pltpu.VMEM(kern.shape, BF16),
            pltpu.VMEM(pairs.shape, BF16),
            pltpu.VMEM(pairs.shape, BF16),
            pltpu.VMEM((2, nx + 1, 2, nz, ny, ch), BF16),
            pltpu.VMEM((2, 2 * ch, 12 * ch), BF16),
            pltpu.SemaphoreType.DMA((5,)),
        ],
        compiler_params=pltpu.CompilerParams(vmem_limit_bytes=56 << 20),
        cost_estimate=pl.CostEstimate(flops=12 * 2**30, bytes_accessed=8 << 20, transcendentals=0),
        name="forward",
    )(upper, low, ylo, yhi, xlo, xhi, kern, bias_row, pairs)
    return out.reshape(2 * nx, nz, 2 * ny, ch), dpre, keep, give, bgrad


def backward_body(dpre, cols, ccols, kern, bias, grad, df, ds, wb, gh, wt):
    build_weights(kern, wt)
    _, duals, _, nz, ny, ch = dpre.shape
    nx = duals - 1
    half = ch // 2
    lanes = gh.shape[3]
    bias_row = jnp.concatenate([bias[...], bias[...]], axis=1)
    for py in range(2):
        pieces = []
        for ux in range(2):
            for vy in range(2):
                which = ((3, 2), (0, 1))[py][vy]
                for dz in range(3):
                    pieces.append(cols[which, dz:dz + nz, ux:ux + lanes, :].reshape(nz * lanes, ch).astype(BF16))
        pre = dot_nt(jnp.concatenate(pieces, axis=1), wt[py])
        for px in range(2):
            part = pre[:, px * ch:(px + 1) * ch] + bias_row
            cots = ccols[py, px].reshape(nz * lanes, ch)
            gh[py, px] = (cots * jnp.where(part > 0, 1.0, SLOPE)).astype(BF16).astype(F32).reshape(nz, lanes, ch)
    zero = jnp.zeros((nx + 1, 2, ny, ch), BF16)
    for var in range(4):
        ds[var, 0] = zero
        ds[var, nz + 1] = zero

    def layer_load(z, carry):
        for py in range(2):
            df[py, :, :, 8:8 + ny, :] = dpre[py, :, :, z].astype(F32)
            for px in range(2):
                df[py, :, px, 7 if py else 8 + ny, :] = gh[py, px, z, 0:nx + 1]
        for py in range(2):
            for vy in range(2):
                lead = 8 if vy == 0 else (9 if py == 0 else 7)
                ds[py * 2 + vy, 1 + z] = df[py, :, :, lead:lead + ny, :].astype(BF16)
        return carry

    lax.fori_loop(0, nz, layer_load, 0, unroll=2)
    for py in range(2):
        for vy in range(2):
            for q in range(4):
                row = ((py * 2 + vy) * 4 + q) * 2 * ch
                ty = TAP_Y[py][vy]
                for place, tz in enumerate((1, 2, 3, 0)):
                    at = row + place * half
                    wb[at:at + half, :] = kern[q, ty, tz]
    lane = lax.broadcasted_iota(jnp.int32, (nx, ny, ch), 2)

    def layer_step(z, carry):
        acc = jnp.zeros((nx * ny, ch), F32)
        for var in range(4):
            pieces = []
            for q in range(4):
                same = ds[var, 1 + z, q // 2:q // 2 + nx, q % 2]
                above = ds[var, 2 + z, q // 2:q // 2 + nx, q % 2]
                below = ds[var, z, q // 2:q // 2 + nx, q % 2]
                mixed = jnp.where(lane < half, above.astype(F32), below.astype(F32)).astype(BF16)
                pieces += [same.reshape(nx * ny, ch), mixed.reshape(nx * ny, ch)]
            acc = acc + jnp.dot(jnp.concatenate(pieces, axis=1), wb[var * 8 * ch:(var + 1) * 8 * ch, :], preferred_element_type=F32)
        grad[:, z] = acc.astype(BF16).reshape(nx, ny, ch)
        return carry

    lax.fori_loop(0, nz, layer_step, 0, unroll=True)


def run_backward(dpre, cols, ccols, kern, bias_row):
    _, duals, _, nz, ny, ch = dpre.shape
    nx = duals - 1
    vmem = pl.BlockSpec(memory_space=pltpu.VMEM)
    return pl.pallas_call(
        backward_body,
        out_shape=jax.ShapeDtypeStruct((nx, nz, ny, ch), BF16),
        in_specs=[vmem] * 5,
        out_specs=vmem,
        scratch_shapes=[
            pltpu.VMEM((2, nx + 1, 2, ny + 16, ch), F32),
            pltpu.VMEM((4, nz + 2, nx + 1, 2, ny, ch), BF16),
            pltpu.VMEM((32 * ch, ch), BF16),
            pltpu.VMEM((2, 2, nz, nx + 8, ch), F32),
            pltpu.VMEM((2, 2 * ch, 12 * ch), BF16),
        ],
        compiler_params=pltpu.CompilerParams(vmem_limit_bytes=40 << 20),
        cost_estimate=pl.CostEstimate(flops=4 * 2**30, bytes_accessed=4 << 20, transcendentals=0),
        name="backward",
    )(dpre, cols, ccols, kern, bias_row)


def from_both(first, last, axis):
    count = lax.axis_size(axis)
    odd = lax.axis_index(axis) % 2 == 1
    inner = lax.ppermute(jnp.where(odd, first, last), axis, [(i, i ^ 1) for i in range(count)])
    other = jnp.where(odd, last, first)
    outer = lax.ppermute(other, axis, [(i, i + 1 if i % 2 else i - 1) for i in range(1, count - 1)])
    return jnp.where(odd, inner, outer), jnp.where(odd, outer, inner)


HALVE = (("gy", 1), ("gy", 4), ("gy", 2))
GROUPS = (("gy", (8,)), ("gx", (1, 8, 9)), ("gx", (2, 5, 7)))


def swap(values, axis, bits):
    return lax.ppermute(values, axis, [(i, i ^ bits) for i in range(lax.axis_size(axis))])


def rounded(values):
    return lax.reduce_precision(values, 8, 7)


def with_extra(values, extra):
    high = rounded(extra)
    tail = [jnp.broadcast_to(part.astype(BF16), (8,) + part.shape[1:]) for part in (high, rounded(extra - high))]
    return jnp.concatenate([values.astype(BF16)] + tail, axis=0), high + rounded(extra - high)


def take_extra(message):
    rows = message.shape[0] - 16
    wide = message.astype(F32)
    return wide[:rows], wide[rows:rows + 1] + wide[rows + 8:rows + 9]


def sum_over_devices(keep, message, brow):
    steps = [(axis, bit) for axis, bit in HALVE if bit < lax.axis_size(axis)]
    groups = [(axis, [bits for bits in some if bits < lax.axis_size(axis)]) for axis, some in GROUPS]
    extra = brow[0:1]
    for at, (axis, bit) in enumerate(steps):
        if at:
            half = part.shape[0] // 2
            up = (lax.axis_index(axis) & bit) != 0
            keep = jnp.where(up, part[half:], part[:half])
            message, extra = with_extra(jnp.where(up, part[:half], part[half:]), extra)
        came, came_extra = take_extra(swap(message, axis, bit))
        part = keep + came
        extra = extra + came_extra
    for axis, some in groups:
        own = rounded(part)
        message, own_extra = with_extra(own, extra)
        arrived = [take_extra(swap(message, axis, bits)) for bits in some]
        if len(arrived) == 3:
            part = (own + arrived[0][0]) + (arrived[1][0] + arrived[2][0])
            extra = (own_extra + arrived[0][1]) + (arrived[1][1] + arrived[2][1])
        else:
            for more, more_extra in arrived:
                part, extra = own + more, own_extra + more_extra
    grown = part.astype(BF16)
    for axis, bit in steps[::-1]:
        up = (lax.axis_index(axis) & bit) != 0
        came = swap(grown, axis, bit)
        grown = jnp.concatenate([jnp.where(up, came, grown), jnp.where(up, grown, came)], axis=0)
    return grown.astype(F32), extra


def per_device(low_res, kernel, bias, cotangent):
    low = jnp.transpose(low_res, (0, 2, 1, 3))
    cot = jnp.transpose(cotangent, (0, 2, 1, 3))
    nx, nz, ny, ch = low.shape
    bias_row = bias.reshape(1, -1)

    first = jnp.concatenate([low[:, :, 0], cot[:, :, 0]], axis=0)
    last = jnp.concatenate([low[:, :, ny - 1], cot[:, :, 2 * ny - 1]], axis=0)
    ylo, yhi = from_both(first, last, "gy")

    def row(cell, output):
        pieces = [cot[output], ylo[cell][:, None], low[cell], yhi[cell][:, None], ylo[nx + output][:, None], yhi[nx + output][:, None]]
        return jnp.concatenate(pieces, axis=1)

    xlo, xhi = from_both(row(0, 0), row(nx - 1, 2 * nx - 1), "gx")
    axis, bit = HALVE[0]
    upper = (lax.axis_index(axis) // bit % 2).astype(jnp.int32).reshape(1)
    out, dpre, keep, give, bgrad = run_forward(upper, low, ylo, yhi, xlo, xhi, kernel, bias_row, cot)

    def column(at, middle):
        first, last = xlo[:, at][:, None], xhi[:, at][:, None]
        return jnp.concatenate([first, jnp.transpose(middle, (1, 0, 2)), last], axis=1)

    cols = jnp.stack([column(2 * ny, ylo[:nx]), column(2 * ny + 1, low[:, :, 0]), column(3 * ny, low[:, :, ny - 1]), column(3 * ny + 1, yhi[:nx])])
    cols = jnp.pad(cols.astype(F32), ((0, 0), (1, 1), (0, 14), (0, 0)))
    ccols = jnp.stack([column(3 * ny + 3, yhi[nx:]), column(3 * ny + 2, ylo[nx:])]).astype(F32)
    ccols = jnp.transpose(ccols.reshape(2, nz, nx + 1, 2, ch), (0, 3, 1, 2, 4))
    ccols = jnp.pad(ccols, ((0, 0), (0, 0), (0, 0), (0, 7), (0, 0)))
    grad = run_backward(dpre, cols, ccols, kernel, bias_row)
    kernel_sum, bias_sum = sum_over_devices(keep, give, bgrad)

    grid_rows = lax.axis_size("gx") * nx
    output = jnp.transpose(out, (0, 2, 1, 3))
    input_grad = jnp.transpose(grad, (0, 2, 1, 3))
    kernel_grad = kernel_sum.reshape(kernel.shape) / grid_rows
    bias_grad = jnp.sum(bias_sum.reshape(2, ch // 2), axis=0) / grid_rows
    return (output, input_grad, kernel_grad, bias_grad)


def solution(mesh):
    return jax.shard_map(
        per_device,
        mesh=mesh,
        in_specs=(P("gx", "gy", None, None), P(), P(), P("gx", "gy", None, None)),
        out_specs=(P("gx", "gy", None, None), P("gx", "gy", None, None), P(), P()),
        check_vma=False,
    )
```
